256 devices in a mesh: dp: 4 (over y_lo, core), mp: 64 (over z, x, y_hi).
Axes of the slice: x: 4, y: 4 (y_hi: 2, y_lo: 2; y = y_hi * 2 + y_lo), z: 8, core: 2. Of those that a mesh axis runs over, the one named last changes fastest.
Arguments:
- features: bfloat16 [4096, 65536], P('dp', 'mp'), may hold values from -6 to 6
- cotangent: bfloat16 [4096, 65536], P('dp', 'mp'), may hold values from -6 to 6
- factor_one: bfloat16 [256, 256, 256], P('mp', 'dp'), may hold values from -0.375 to 0.375
- factor_two: bfloat16 [256, 256, 256], P('mp', 'dp'), may hold values from -0.375 to 0.375
Outputs:
- layer_out: bfloat16 [4096, 65536], P('dp', 'mp')
- grad_input: bfloat16 [4096, 65536], P('dp', 'mp')
- grad_one: float32 [256, 256, 256], P('mp', 'dp')
- grad_two: float32 [256, 256, 256], P('mp', 'dp')
The draws below stay inside these ranges and needn't reach their ends.
All inputs are finite; a program needn't handle non-finite values.
Results may differ from the reference program's by a relative error of at most 0.0095.
Values may be sent and summed in bfloat16 or wider, within the bound.
A program may use at most 64 MiB of HBM per device.

```python
import math
import jax
import jax.numpy as jnp
from jax import lax

NB = 256
BS = 256
WIDTH = 65536
TOKENS = 4096


def steps_of(rng, shape, shards, smallest, high):
    factor_of, own = 1.0, jax.random.fold_in(rng, 6)
    for position, blocks in shards:
        draws = jnp.exp(jax.random.uniform(jax.random.fold_in(own, position), (blocks,), jnp.float32, smallest / len(shards), high / len(shards)))
        factor_of = factor_of * jnp.repeat(draws, shape[position] // blocks).reshape([-1 if axis == position else 1 for axis in range(len(shape))])
    return factor_of


def noise(key, dims, scale, bound, cuts=(), held_as=jnp.bfloat16):
    result = scale * jax.random.normal(key, dims, jnp.float32)
    if cuts:
        result = result * steps_of(key, dims, cuts, -0.22, 0.18)
    return jnp.clip(result, -bound, bound).astype(held_as)


def setup_inputs(seed: int = 0) -> dict:
    keys = jax.random.split(jax.random.key(seed), 5)
    features = noise(keys[0], (TOKENS, WIDTH), 1.0, 6.0, ((0, 4), (1, 64)))
    cotangent = noise(keys[1], (TOKENS, WIDTH), 1.0, 6.0, ((0, 4), (1, 64)))
    factor_one = noise(keys[2], (NB, BS, BS), BS ** -0.5, 0.375, ((0, 64), (1, 4)))
    factor_two = noise(keys[3], (BS, NB, NB), NB ** -0.5, 0.375, ((0, 64), (1, 4)))
    return dict(features=features, cotangent=cotangent, factor_one=factor_one, factor_two=factor_two)


def gelu_value(value):
    inner = math.sqrt(2.0 / math.pi) * (value + 0.044715 * value * value * value)
    return 0.5 * value * (1.0 + jnp.tanh(inner))

def gelu_slope(value):
    scale = math.sqrt(2.0 / math.pi)
    tangent = jnp.tanh(scale * (value + 0.044715 * value * value * value))
    return 0.5 * (1.0 + tangent) + 0.5 * value * (1.0 - tangent * tangent) * scale * (1.0 + 3.0 * 0.044715 * value * value)

def reference(features, cotangent, factor_one, factor_two):
    block_rows = 512 if TOKENS % 512 == 0 else TOKENS
    count = TOKENS // block_rows
    w_one = factor_one.astype(jnp.float32)
    w_two = factor_two.astype(jnp.float32)

    def advance(carry, pair):
        rows_in, rows_cot = pair
        blocks_in = rows_in.reshape(block_rows, NB, BS).astype(jnp.float32)
        first = jnp.einsum('tbi,bij->tbj', blocks_in, w_one).astype(jnp.bfloat16)
        preact = jnp.einsum('tbj,jbk->tjk', first.astype(jnp.float32), w_two)
        layer_out = (rows_in.astype(jnp.float32) + gelu_value(preact).reshape(block_rows, -1)).astype(jnp.bfloat16)
        cot_blocks = rows_cot.astype(jnp.float32).reshape(block_rows, BS, NB)
        slope = (cot_blocks * gelu_slope(preact)).astype(jnp.bfloat16)
        back_first = jnp.einsum('tjk,jbk->tbj', slope.astype(jnp.float32), w_two).astype(jnp.bfloat16)
        grad_input = (rows_cot.astype(jnp.float32) + jnp.einsum('tbj,bij->tbi', back_first.astype(jnp.float32), w_one).reshape(block_rows, -1)).astype(jnp.bfloat16)
        grad_one = carry[0] + jnp.einsum('tbi,tbj->bij', blocks_in, back_first.astype(jnp.float32))
        grad_two = carry[1] + jnp.einsum('tbj,tjk->jbk', first.astype(jnp.float32), slope.astype(jnp.float32))
        return ((grad_one, grad_two), (layer_out, grad_input))
    start = (jnp.zeros((NB, BS, BS), jnp.float32), jnp.zeros((BS, NB, NB), jnp.float32))
    stacked = (features.reshape(count, block_rows, NB * BS), cotangent.reshape(count, block_rows, NB * BS))
    grads, outputs = lax.scan(advance, start, stacked)
    layer_out = outputs[0].reshape(TOKENS, NB * BS)
    grad_input = outputs[1].reshape(TOKENS, NB * BS)
    return (layer_out, grad_input, grads[0], grads[1])
```

```python
import functools
import math

import jax
import jax.numpy as jnp
from jax import lax
from jax.experimental import pallas as pl
from jax.experimental.pallas import tpu as pltpu
from jax.sharding import PartitionSpec as P

MESH = pl.DeviceIdType.MESH
BF16 = jnp.bfloat16
F32 = jnp.float32
CHUNKS = 4

NT = (((1,), (1,)), ((), ()))
TN = (((0,), (0,)), ((), ()))
NN = (((1,), (0,)), ((), ()))


def dot(a, b, dims):
    return lax.dot_general(a, b, dims, preferred_element_type=F32)


def gelu_both(v):
    scale = math.sqrt(2.0 / math.pi)
    sq = v * v
    t = jnp.tanh(scale * (v + 0.044715 * sq * v))
    half = 0.5 * (1.0 + t)
    value = v * half
    slope = half + 0.5 * v * (1.0 - t * t) * scale * (1.0 + 3.0 * 0.044715 * sq)
    return value, slope


def kernel(
    groups,
    shards,
    x_hbm,
    c_hbm,
    w1_hbm,
    w2_hbm,
    lay_hbm,
    gin_hbm,
    g1_hbm,
    g2_hbm,
    x_ref,
    c_ref,
    lay_ref,
    gin_ref,
    slope_ref,
    w1_ref,
    w2_ref,
    w1x_ref,
    w2x_ref,
    perm_ref,
    pick_ref,
    s1_ref,
    r1_ref,
    s2_ref,
    r2_ref,
    f_ref,
    acc1_ref,
    acc2_ref,
    p1_ref,
    p2_ref,
    q1_ref,
    q2_ref,
    o1_ref,
    o2_ref,
    in_sem,
    w_sem,
    send_sem,
    r1_sem,
    r2_sem,
    q_sem,
    out_sem,
):
    me = lax.axis_index("mp")
    my = lax.axis_index("dp")
    tokens, width = x_ref.shape
    local = width // 256
    tc = tokens // CHUNKS
    own = 256 // shards
    rows = local * local

    load_x = pltpu.make_async_copy(x_hbm, x_ref, in_sem.at[0])
    load_c = pltpu.make_async_copy(c_hbm, c_ref, in_sem.at[1])
    load_x.start()
    load_c.start()

    barrier = pltpu.get_barrier_semaphore()

    def greet(step, _):
        pl.semaphore_signal(
            barrier, inc=1, device_id=(my, lax.rem(me + step, groups)), device_id_type=MESH
        )
        return 0

    def greet_dp(step, _):
        pl.semaphore_signal(
            barrier, inc=1, device_id=(lax.rem(my + step, shards), me), device_id_type=MESH
        )
        return 0

    lax.fori_loop(1, shards, greet_dp, 0)
    lax.fori_loop(1, groups, greet, 0)

    def build(i, _):
        r0 = pl.multiple_of(i * 128, 128)
        row = lax.broadcasted_iota(jnp.int32, (128, 256), 0) + r0
        col = lax.broadcasted_iota(jnp.int32, (128, 256), 1)
        m4 = lax.shift_right_logical(row, 4) * 4
        u = lax.bitwise_and(lax.shift_right_logical(row, 2), 3)
        v = lax.bitwise_and(row, 3)
        for q in range(local):
            pick_ref[pl.ds(r0, 128), q * 256 : (q + 1) * 256] = jnp.where(
                jnp.logical_and(v == q, col == m4 + u), 1.0, 0.0
            ).astype(BF16)
            perm_ref[pl.ds(r0, 128), q * 256 : (q + 1) * 256] = jnp.where(
                jnp.logical_and(u == q, col == m4 + v), 1.0, 0.0
            ).astype(BF16)
        return 0

    lax.fori_loop(0, width // 128, build, 0)

    pl.semaphore_wait(barrier, groups - 1 + shards - 1)

    mine = pl.ds(pl.multiple_of(my * own, own), own)
    for n, (w_hbm, w_ref) in enumerate(((w1_hbm, w1_ref), (w2_hbm, w2_ref))):
        pltpu.make_async_copy(w_hbm, w_ref.at[:, mine, :], w_sem.at[n]).start()
        for step in range(1, shards):
            pltpu.make_async_remote_copy(
                src_ref=w_hbm,
                dst_ref=w_ref.at[:, mine, :],
                send_sem=send_sem.at[n],
                recv_sem=w_sem.at[n],
                device_id=(lax.rem(my + step, shards), me),
                device_id_type=MESH,
            ).start()

    def scatter(src, dst, c, ssem, rsem):
        here = pl.ds(pl.multiple_of(me * rows, rows), rows)
        pltpu.make_async_copy(src.at[c, here, :], dst.at[c, here, :], rsem.at[c]).start()

        def send(step, _):
            to = lax.rem(me + step, groups)
            pltpu.make_async_remote_copy(
                src_ref=src.at[c, pl.ds(pl.multiple_of(to * rows, rows), rows), :],
                dst_ref=dst.at[c, here, :],
                send_sem=ssem,
                recv_sem=rsem.at[c],
                device_id=(my, to),
                device_id_type=MESH,
            ).start()
            return 0

        lax.fori_loop(1, groups, send, 0)

    def expand(out_ref, w_ref, dims):
        for q in range(local):
            w = w_ref[q]
            for i in range(4):
                part = slice(i * 256, (i + 1) * 256)
                out_ref[part, q * 256 : (q + 1) * 256] = dot(
                    pick_ref[part, q * 256 : (q + 1) * 256], w, dims
                ).astype(BF16)

    load_x.wait()
    pltpu.make_async_copy(w1_ref, w1_ref, w_sem.at[0]).wait()
    expand(w1x_ref, w1_ref, NT)

    def first_stage(c, _):
        here = pl.ds(pl.multiple_of(c * tc, tc), tc)
        for i in range(4):
            part = slice(i * 256, (i + 1) * 256)
            s1_ref[c, part, :] = dot(w1x_ref[part, :], x_ref[here, :], NT).astype(BF16)
        scatter(s1_ref, r1_ref, c, send_sem.at[2], r1_sem)
        return 0

    lax.fori_loop(0, CHUNKS, first_stage, 0)

    pltpu.make_async_copy(w2_ref, w2_ref, w_sem.at[1]).wait()
    expand(w2x_ref, w2_ref, NN)
    acc1_ref[...] = jnp.zeros_like(acc1_ref)
    acc2_ref[...] = jnp.zeros_like(acc2_ref)
    load_c.wait()

    def second_stage(c, _):
        here = pl.ds(pl.multiple_of(c * tc, tc), tc)
        pltpu.make_async_copy(r1_ref.at[c], r1_ref.at[c], r1_sem.at[c]).wait()
        got = r1_ref[c].T
        for q in range(local):
            cols = slice(q * 256, (q + 1) * 256)
            f = dot(got, perm_ref[:, cols], NN).astype(BF16)
            f_ref[:, cols] = f
            pre = dot(f, w2_ref[q], NN)
            value, slope = gelu_both(pre)
            lay_ref[here, cols] = (x_ref[here, cols].astype(F32) + value).astype(BF16)
            slope_ref[here, cols] = (c_ref[here, cols].astype(F32) * slope).astype(BF16)
        for i in range(4):
            part = slice(i * 256, (i + 1) * 256)
            s2_ref[c, part, :] = dot(w2x_ref[part, :], slope_ref[here, :], NT).astype(BF16)
        scatter(s2_ref, r2_ref, c, send_sem.at[3], r2_sem)
        pltpu.make_async_copy(lay_ref.at[here, :], lay_hbm.at[here, :], out_sem.at[0]).start()
        for q in range(local):
            cols = slice(q * 256, (q + 1) * 256)
            acc2_ref[q] += dot(f_ref[:, cols], slope_ref[here, cols], TN)
        return 0

    lax.fori_loop(0, CHUNKS, second_stage, 0)

    def reduce_start(n, acc_ref, p_ref, q_ref):
        p_ref[...] = acc_ref[...].astype(BF16)
        pltpu.make_async_copy(p_ref.at[:, mine, :], q_ref.at[my], q_sem.at[n]).start()
        for step in range(1, shards):
            to = lax.rem(my + step, shards)
            pltpu.make_async_remote_copy(
                src_ref=p_ref.at[:, pl.ds(pl.multiple_of(to * own, own), own), :],
                dst_ref=q_ref.at[my],
                send_sem=send_sem.at[4 + n],
                recv_sem=q_sem.at[n],
                device_id=(to, me),
                device_id_type=MESH,
            ).start()

    def reduce_end(n, q_ref, o_ref, g_hbm):
        pltpu.make_async_copy(q_ref, q_ref, q_sem.at[n]).wait()
        total = q_ref[0].astype(F32)
        for s in range(1, shards):
            total = total + q_ref[s].astype(F32)
        o_ref[...] = total
        pltpu.make_async_copy(o_ref, g_hbm, out_sem.at[2 + n]).start()

    reduce_start(1, acc2_ref, p2_ref, q2_ref)

    def last_stage(c, _):
        here = pl.ds(pl.multiple_of(c * tc, tc), tc)
        pltpu.make_async_copy(r2_ref.at[c], r2_ref.at[c], r2_sem.at[c]).wait()
        got = r2_ref[c].T
        for q in range(local):
            cols = slice(q * 256, (q + 1) * 256)
            f = dot(got, perm_ref[:, cols], NN).astype(BF16)
            acc1_ref[q] += dot(x_ref[here, cols], f, TN)
            through = dot(f, w1_ref[q], NT)
            gin_ref[here, cols] = (c_ref[here, cols].astype(F32) + through).astype(BF16)
        pltpu.make_async_copy(gin_ref.at[here, :], gin_hbm.at[here, :], out_sem.at[1]).start()
        return 0

    lax.fori_loop(0, CHUNKS - 1, last_stage, 0)
    reduce_end(1, q2_ref, o2_ref, g2_hbm)
    last_stage(CHUNKS - 1, 0)
    reduce_start(0, acc1_ref, p1_ref, q1_ref)
    reduce_end(0, q1_ref, o1_ref, g1_hbm)

    for n, w_hbm in enumerate((w1_hbm, w2_hbm)):
        for _ in range(1, shards):
            pltpu.make_async_copy(w_hbm, w_hbm, send_sem.at[n]).wait()
    others = pl.ds(0, (groups - 1) * rows)
    for n, s_ref in ((2, s1_ref), (3, s2_ref)):
        for c in range(CHUNKS):
            pltpu.make_async_copy(
                s_ref.at[c, others, :], s_ref.at[c, others, :], send_sem.at[n]
            ).wait()
    for n, p_ref in enumerate((p1_ref, p2_ref)):
        part = p_ref.at[:, pl.ds(0, (shards - 1) * own), :]
        pltpu.make_async_copy(part, part, send_sem.at[4 + n]).wait()
    pltpu.make_async_copy(lay_ref, lay_hbm, out_sem.at[0]).wait()
    pltpu.make_async_copy(gin_ref, gin_hbm, out_sem.at[1]).wait()
    pltpu.make_async_copy(o1_ref, g1_hbm, out_sem.at[2]).wait()
    pltpu.make_async_copy(o2_ref, g2_hbm, out_sem.at[3]).wait()


def on_device(features, cotangent, factor_one, factor_two):
    groups, shards = lax.axis_size("mp"), lax.axis_size("dp")
    tokens, width = features.shape
    tc = tokens // CHUNKS
    local = width // 256
    big = pltpu.VMEM((tokens, width), BF16)
    square = pltpu.VMEM((width, width), BF16)
    message = pltpu.VMEM((CHUNKS, width, tc), BF16)
    blocks = (local, 256, 256)
    anywhere = pl.BlockSpec(memory_space=pl.ANY)
    return pl.pallas_call(
        functools.partial(kernel, groups, shards),
        out_shape=(
            jax.ShapeDtypeStruct(features.shape, BF16),
            jax.ShapeDtypeStruct(features.shape, BF16),
            jax.ShapeDtypeStruct(factor_one.shape, F32),
            jax.ShapeDtypeStruct(factor_two.shape, F32),
        ),
        in_specs=[anywhere] * 4,
        out_specs=(anywhere,) * 4,
        scratch_shapes=[
            big,
            big,
            big,
            big,
            big,
            pltpu.VMEM(blocks, BF16),
            pltpu.VMEM(blocks, BF16),
            square,
            square,
            square,
            square,
            message,
            message,
            message,
            message,
            pltpu.VMEM((tc, width), BF16),
            pltpu.VMEM(blocks, F32),
            pltpu.VMEM(blocks, F32),
            pltpu.VMEM(blocks, BF16),
            pltpu.VMEM(blocks, BF16),
            pltpu.VMEM((shards,) + factor_one.shape, BF16),
            pltpu.VMEM((shards,) + factor_one.shape, BF16),
            pltpu.VMEM(factor_one.shape, F32),
            pltpu.VMEM(factor_one.shape, F32),
            pltpu.SemaphoreType.DMA((2,)),
            pltpu.SemaphoreType.DMA((2,)),
            pltpu.SemaphoreType.DMA((6,)),
            pltpu.SemaphoreType.DMA((CHUNKS,)),
            pltpu.SemaphoreType.DMA((CHUNKS,)),
            pltpu.SemaphoreType.DMA((2,)),
            pltpu.SemaphoreType.DMA((4,)),
        ],
        compiler_params=pltpu.CompilerParams(
            collective_id=0, has_side_effects=True, vmem_limit_bytes=56 * 2**20
        ),
        name="monarch",
    )(features, cotangent, factor_one, factor_two)


def solution(mesh):
    in_specs = (P("dp", "mp"), P("dp", "mp"), P("mp", "dp", None), P("mp", "dp", None))
    out_specs = (P("dp", "mp"), P("dp", "mp"), P("mp", "dp", None), P("mp", "dp", None))
    return jax.shard_map(
        on_device, mesh=mesh, in_specs=in_specs, out_specs=out_specs, check_vma=False
    )
```
